128 devices in a mesh: prow: 16 (over z, x), pcol: 8 (over y, core).
Axes of the slice: x: 4, y: 4, z: 4, core: 2. Of those that a mesh axis runs over, the one named last changes fastest.
Arguments:
- kernel_tiles: float32 [4, 16, 256, 8, 8, 256], P(None, 'prow', None, None, 'pcol'), may hold values from 0 to 11, as said below
Outputs:
- factored: float32 [4, 16, 256, 8, 8, 256], P(None, 'prow', None, None, 'pcol')
The draws below stay inside these ranges and needn't reach their ends.
Inputs may be any that keep to these rules, and one draw needn't show every extreme that they name: kernel_tiles is a symmetric positive definite matrix in the stated layout: a product of two exponential covariances of locations and times, scaled per point, plus a diagonal term of at least 0.5.
All inputs are finite; a program needn't handle non-finite values.
Results may differ from the reference program's by a relative error of at most 0.000061.
Values sent between devices are 32-bit elements; how exact they have to be, the bound alone decides.
A program may use at most 128 MiB of HBM per device.

```python
import math
import jax
import jax.numpy as jnp
from jax import lax

NB = 256
RT = 4
TILES = 64
CT = 8
ORDER = 16384


def draw_kernel_tiles(key, part):
    streams = jax.random.split(key, 4)
    total = TILES * NB
    place = jax.random.uniform(streams[0], (total,), jnp.float32, 0.0, 16.0)
    moment = jax.random.uniform(streams[1], (total,), jnp.float32, 0.0, 4.0)
    amplitude = jnp.exp(jax.random.uniform(streams[2], (total,), jnp.float32, math.log(0.5), math.log(2.0)))
    nugget = jax.random.uniform(streams[3], (total,), jnp.float32, 0.5, 1.5)
    distance = jnp.abs(place[:, None] - place[None, :]) + jnp.abs(moment[:, None] - moment[None, :])
    matrix = amplitude[:, None] * amplitude[None, :] * jnp.exp(-distance) + jnp.diag(nugget)
    return matrix.reshape(RT, TILES // RT, NB, CT, TILES // CT, NB)


def setup_inputs(seed: int = 0) -> dict:
    keys = jax.random.split(jax.random.key(seed), 2)
    kernel_tiles = draw_kernel_tiles(jax.random.fold_in(keys[1], 71), 0)
    return {"kernel_tiles": kernel_tiles}


def reference(kernel_tiles):
    matrix = kernel_tiles.reshape(ORDER, ORDER)
    first = jnp.linalg.cholesky(matrix[:NB, :NB])
    left = jax.scipy.linalg.solve_triangular(first, matrix[NB:, :NB].T, lower=True).T
    schur = matrix[NB:, NB:] - jnp.dot(left, left.T, precision=lax.Precision.HIGHEST)
    second = jnp.linalg.cholesky(schur[:NB, :NB])
    lower_part = jax.scipy.linalg.solve_triangular(second, schur[NB:, :NB].T, lower=True).T
    remainder = schur[NB:, NB:] - jnp.dot(lower_part, lower_part.T, precision=lax.Precision.HIGHEST)
    result = jnp.zeros((ORDER, ORDER), jnp.float32)
    result = result.at[:, :NB].set(jnp.concatenate([first, left], axis=0))
    result = result.at[NB:, NB:2 * NB].set(jnp.concatenate([second, lower_part], axis=0))
    result = result.at[2 * NB:, 2 * NB:].set(remainder)
    return result.reshape(kernel_tiles.shape)
```

```python
import functools

import jax
import jax.numpy as jnp
from jax import lax
from jax.experimental import pallas as pl
from jax.experimental.pallas import tpu as pltpu
from jax.sharding import PartitionSpec as P

MESH = pl.DeviceIdType.MESH
HI = lax.Precision.HIGHEST
F = jnp.float32
BF = jnp.bfloat16
NB = 256
SB = 128
SIDE = 4

TREE = {
    (0, 1): (1, 0), (3, 0): (-1, 0), (0, 3): (1, 0), (1, 0): (-1, 0), (0, 2): (1, 0),
    (2, 0): (-1, 0), (1, 1): (-1, 0), (3, 1): (0, 1), (3, 3): (0, -1), (1, 3): (-1, 0),
    (1, 2): (-1, 0), (2, 1): (0, 1), (3, 2): (0, -1), (2, 3): (-1, 0), (2, 2): (0, 1),
}
STEPS = ((1, 0), (-1, 0), (0, 1), (0, -1))
CHUNKS = 4


def tree_parents():
    trees = [TREE]
    for _ in range(3):
        trees.append({((-x) % SIDE, z): (-s, d) for (z, x), (d, s) in trees[-1].items()})
    return trees


def children(tree, step):
    return [
        (v[0] - step[0]) % SIDE * SIDE + (v[1] - step[1]) % SIDE
        for v, d in tree.items()
        if d == step
    ]


def one_of(value, options):
    found = value == options[0]
    for other in options[1:]:
        found = found | (value == other)
    return found


def factor_block(x, after_leaf):
    n = x.shape[0]
    leaves = n // 8
    rows = [x[8 * i : 8 * i + 8] for i in range(leaves)]
    lane = lax.broadcasted_iota(jnp.int32, (8, n), 1)
    sub = lax.broadcasted_iota(jnp.int32, (8, n), 0)
    out = []
    for b in range(leaves):
        o = 8 * b
        c = [jnp.broadcast_to(rows[b][:, o + k : o + k + 1], (8, n)) for k in range(8)]
        inside = (lane >= o) & (lane < o + 8)
        g = jnp.where(inside, jnp.where(lane - o == sub, F(1), F(0)), rows[b])
        r = jnp.zeros_like(g)
        for j in range(8):
            pivot = jnp.broadcast_to(c[j][j : j + 1], (8, n))
            inv = 1.0 / pivot
            row = jnp.broadcast_to(g[j : j + 1], (8, n))
            here = sub == j
            r = jnp.where(here, row * lax.rsqrt(pivot), r)
            grow = row * inv
            g = jnp.where(here, grow, g - c[j] * grow)
            for k in range(j + 1, 8):
                ck = jnp.broadcast_to(c[k][j : j + 1], (8, n)) * inv
                c[k] = jnp.where(here, ck, c[k] - c[j] * ck)
        out.append(r)
        if b + 1 < leaves:
            below = rows[b + 1]
            acc = jnp.where(inside, F(0), below)
            for k in range(8):
                acc = acc - jnp.broadcast_to(below[:, o + k : o + k + 1], (8, n)) * jnp.broadcast_to(
                    g[k : k + 1], (8, n)
                )
            rows[b + 1] = acc
        if b + 2 < leaves:
            rest = jnp.concatenate(rows[b + 2 :], axis=0)
            parts = [g, jnp.zeros((n - o - 8, n), F)]
            if o:
                parts = [jnp.zeros((o, n), F)] + parts
            lanes = lax.broadcasted_iota(jnp.int32, rest.shape, 1)
            cleared = jnp.where((lanes >= o) & (lanes < o + 8), F(0), rest)
            rest = cleared - jnp.dot(rest, jnp.concatenate(parts, axis=0), precision=HI, preferred_element_type=F)
            for i in range(b + 2, leaves):
                rows[i] = rest[8 * (i - b - 2) : 8 * (i - b - 2) + 8]
        after_leaf()
    return jnp.concatenate(out, axis=0)


def factor_all(d_ref, w_ref, after_leaf, after_first):
    n = w_ref.shape[0]
    li = lax.broadcasted_iota(jnp.int32, (SB, SB), 1)
    si = lax.broadcasted_iota(jnp.int32, (SB, SB), 0)
    for r0 in range(0, n, SB):
        src = w_ref if r0 else d_ref
        here = pl.ds(r0, SB)
        f = factor_block(src[here, here], after_leaf)
        if not r0:
            after_first()
        w = jnp.where(li <= si, f, F(0))
        w_ref[here, :] = jnp.dot(w, src[here, :], precision=HI, preferred_element_type=F)
        w_ref[here, here] = w
        k0 = r0 + SB
        if k0 < n:
            rr = w_ref[here, :]
            upd = lax.dot_general(
                rr[:, k0:], rr, (((0,), (0,)), ((), ())), precision=HI, preferred_element_type=F
            )
            col = lax.broadcasted_iota(jnp.int32, (n - k0, n), 1)
            old = jnp.where((col >= r0) & (col < k0), F(0), src[pl.ds(k0, n - k0), :])
            w_ref[pl.ds(k0, n - k0), :] = old - upd
            w_ref[here, pl.ds(k0, n - k0)] = jnp.zeros((SB, n - k0), F)


def gather_kernel(x_ref, a_ref, t_ref, r_ref, w_ref, d_ref, sem_local, sem_stage, t_send, t_recv, r_send, r_recv, d_send, d_recv):
    p = lax.axis_index("prow")
    q = lax.axis_index("pcol")
    z, x = p // SIDE, p % SIDE
    y, c = q // 2, q % 2
    tiles = x_ref.shape[3]
    row_tiles = x_ref.shape[0]

    def dev(dz=0, dx=0, dy=0, other=False):
        cc = 1 - c if other else c
        return {
            "prow": (z + dz + SIDE) % SIDE * SIDE + (x + dx + SIDE) % SIDE,
            "pcol": (y + dy + SIDE) % SIDE * 2 + cc,
        }

    stage = []
    for k in range(2):
        for j in range(tiles):
            stage.append(
                (
                    p == k,
                    pltpu.make_async_copy(
                        x_ref.at[0, 0, :, j, 0, :],
                        t_ref.at[pl.ds(NB * k, NB), pl.ds(NB * j, NB)],
                        sem_stage.at[len(stage)],
                    ),
                )
            )
    for row, col in ((0, 0), (0, 1), (1, 1)):
        stage.append(
            (
                (p == row) & (q == col),
                pltpu.make_async_copy(
                    x_ref.at[0, 0, :, 0, 0, :],
                    d_ref.at[pl.ds(NB * row, NB), pl.ds(NB * col, NB)],
                    sem_stage.at[len(stage)],
                ),
            )
        )
    for k in range(2):
        for i in range(row_tiles):
            stage.append(
                (
                    q == k,
                    pltpu.make_async_copy(
                        x_ref.at[i, 0, :, 0, 0, :], r_ref.at[k, pl.ds(NB * i, NB), :], sem_stage.at[len(stage)]
                    ),
                )
            )
    for cond, copy in stage:
        pl.when(cond)(copy.start)
    own = [
        pltpu.make_async_copy(
            x_ref.at[i, 0, :, j, 0, :],
            a_ref.at[pl.ds(NB * i, NB), pl.ds(NB * j, NB)],
            sem_local.at[i * tiles + j],
        )
        for i in range(row_tiles)
        for j in range(tiles)
    ]
    for copy in own:
        copy.start()

    barrier = pltpu.get_barrier_semaphore()
    peers = [dev(other=True)]
    for s in range(1, SIDE):
        peers += [dev(dz=s), dev(dx=s), dev(dy=s)]
    for peer in peers:
        pl.semaphore_signal(barrier, inc=1, device_id=peer, device_id_type=MESH)
    pl.semaphore_wait(barrier, len(peers))
    for cond, copy in stage:
        pl.when(cond)(copy.wait)

    sends = []

    def remote(ref, send, recv, peer):
        return pltpu.make_async_remote_copy(
            src_ref=ref, dst_ref=ref, send_sem=send, recv_sem=recv, device_id=peer, device_id_type=MESH
        )

    def send(cond, copy):
        pl.when(cond)(copy.start)
        sends.append((cond, copy))

    def line(s):
        return ((s == 0, 1), (s == 0, 3), (s == 1, 1))

    pieces = [
        (0, 128, 0, 128, 0, 0),
        (0, 256, 128, 256, 0, 0),
        (0, 256, 256, 512, 0, 1),
        (256, 512, 256, 512, 1, 1),
    ]

    def lead_piece(i):
        ra, rb, ca, cb, x0, c0 = pieces[i]
        ref = d_ref.at[pl.ds(ra, rb - ra), pl.ds(ca, cb - ca)]
        mine = c == c0
        root = mine & (z == 0) & (x == x0) & (y == 0)
        rx = (x - x0 + SIDE) % SIDE

        @pl.when(jnp.logical_not(root))
        def _():
            remote(ref, d_send.at[i, 0], d_recv.at[i], dev(other=True)).wait_recv()

        for j, (cond, step) in enumerate(line(y)):
            send(mine & (z == 0) & (rx == 0) & cond, remote(ref, d_send.at[i, j], d_recv.at[i], dev(dy=step)))
        for j, (cond, step) in enumerate(line(z)):
            send(mine & (rx == 0) & cond, remote(ref, d_send.at[i, 3 + j], d_recv.at[i], dev(dz=step)))
        for j, (cond, step) in enumerate(line(rx)):
            send(mine & cond, remote(ref, d_send.at[i, 6 + j], d_recv.at[i], dev(dx=step)))
        send(mine, remote(ref, d_send.at[i, 9], d_recv.at[i], dev(other=True)))

    def row_chain(i):
        down = i >= row_tiles // 2
        step = SIDE - 1 if down else 1
        for k in range(2):
            ref = r_ref.at[k, pl.ds(NB * i, NB), :]
            mine = c == k
            last = 1 if down else SIDE - 1

            @pl.when(mine & (y != 0))
            def _():
                remote(ref, r_send.at[k, i, 0], r_recv.at[k, i], dev(dy=step)).wait_recv()

            send(mine & (y != last), remote(ref, r_send.at[k, i, 0], r_recv.at[k, i], dev(dy=step)))
            send(mine, remote(ref, r_send.at[k, i, 1], r_recv.at[k, i], dev(other=True)))

    def row_partner(i):
        for k in range(2):
            ref = r_ref.at[k, pl.ds(NB * i, NB), :]

            @pl.when(c != k)
            def _():
                remote(ref, r_send.at[k, i, 1], r_recv.at[k, i], dev(other=True)).wait_recv()

    trees = tree_parents()
    rel = [z * SIDE + (x - k + SIDE) % SIDE for k in range(2)]
    has = [[[one_of(rel[k], children(t, s)) for s in STEPS] for t in trees] for k in range(2)]
    share = NB // len(trees)
    size = share // CHUNKS

    def tree_chunk(k, t, i):
        e = (k * len(trees) + t) * CHUNKS + i
        ref = t_ref.at[pl.ds(NB * k + share * t + size * i, size), :]

        @pl.when(rel[k] != 0)
        def _():
            remote(ref, t_send.at[e, 0], t_recv.at[e], dev(other=True)).wait_recv()

        for j, (dz, dx) in enumerate(STEPS):
            send(has[k][t][j], remote(ref, t_send.at[e, j], t_recv.at[e], dev(dz=dz, dx=dx)))

    todo = [functools.partial(lead_piece, i) for i in range(1, len(pieces))]
    trees_todo = [
        functools.partial(tree_chunk, k, t, i)
        for i in range(CHUNKS)
        for k in range(2)
        for t in range(len(trees))
    ]
    order = [row_tiles // 2, 0, row_tiles // 2 + 1, 1]
    chains = [functools.partial(row_chain, i) for i in order]
    partners = [functools.partial(row_partner, i) for i in order]
    queue = []
    for n, item in enumerate(trees_todo):
        queue.append(item)
        if n % 2 == 1 and chains:
            queue.append(chains.pop(0))
        elif n >= 12 and n % 2 == 1 and partners:
            queue.append(partners.pop(0))

    def after_leaf():
        for _ in range(1 if todo else 2):
            if todo:
                todo.pop(0)()
            elif queue:
                queue.pop(0)()

    lead_piece(0)

    def after_first():
        while todo:
            todo.pop(0)()

    factor_all(d_ref, w_ref, after_leaf, after_first)
    while queue:
        queue.pop(0)()
    for cond, copy in sends:
        pl.when(cond)(copy.wait_send)
    for copy in own:
        copy.wait()


def split(v):
    hi = v.astype(BF)
    return hi, (v - hi.astype(F)).astype(BF)


def dot(a, b):
    return jnp.dot(a, b, preferred_element_type=F)


def update_kernel(a_ref, t_ref, r_ref, w_ref, o_ref, thi, tlo, buf, sem):
    p = lax.axis_index("prow")
    q = lax.axis_index("pcol")
    prows = lax.axis_size("prow")
    tiles = a_ref.shape[1] // NB
    row_tiles = a_ref.shape[0] // NB
    ri = lax.broadcasted_iota(jnp.int32, (NB, NB), 0)
    ci = lax.broadcasted_iota(jnp.int32, (NB, NB), 1)
    for j in range(tiles):
        sl = pl.ds(NB * j, NB)
        hi, lo = split(t_ref[:, sl])
        thi[:, sl] = hi
        tlo[:, sl] = lo

    def copies(i, j):
        return pltpu.make_async_copy(
            buf.at[i % 2, :, pl.ds(NB * j, NB)], o_ref.at[i, 0, :, j, 0, :], sem.at[i % 2, j]
        )

    def body(i, carry):
        rows = pl.ds(pl.multiple_of(i * NB, NB), NB)
        ar = jnp.concatenate([r_ref[0, rows, :], r_ref[1, rows, :]], axis=1)
        w = w_ref[...]
        pr = lax.dot_general(ar, w, (((1,), (1,)), ((), ())), precision=HI, preferred_element_type=F)
        bhi, blo = split(jnp.dot(pr, w, precision=HI, preferred_element_type=F))
        row = i * prows + p
        active = row > 1

        @pl.when(i >= 2)
        def _():
            for j in range(tiles):
                copies(i - 2, j).wait()

        for j in range(tiles):
            sl = pl.ds(NB * j, NB)
            hi, lo = thi[:, sl], tlo[:, sl]
            val = a_ref[rows, sl] - (dot(bhi, hi) + (dot(bhi, lo) + dot(blo, hi)))
            val = jnp.where(active, val, F(0))
            if j == 0:
                panel = jnp.where(q == 0, pr[:, :NB], pr[:, NB:])
                keep = (row > q) | ((row == q) & (ci <= ri))
                val = jnp.where(q < 2, jnp.where(keep, panel, F(0)), val)
            buf[i % 2, :, sl] = val
            copies(i, j).start()
        return carry

    lax.fori_loop(0, row_tiles, body, 0)
    for i in range(row_tiles - 2, row_tiles):
        for j in range(tiles):
            copies(i, j).wait()


def shards(kernel_tiles):
    row_tiles, _, nb, tiles, _, _ = kernel_tiles.shape
    rows, cols, lead = row_tiles * nb, tiles * nb, 2 * nb
    vmem = pl.BlockSpec(memory_space=pltpu.VMEM)
    dma = pltpu.SemaphoreType.DMA
    events = 2 * 4 * CHUNKS
    a, t, r, w = pl.pallas_call(
        gather_kernel,
        out_shape=[
            jax.ShapeDtypeStruct((rows, cols), F),
            jax.ShapeDtypeStruct((lead, cols), F),
            jax.ShapeDtypeStruct((2, rows, nb), F),
            jax.ShapeDtypeStruct((lead, lead), F),
        ],
        in_specs=[pl.BlockSpec(memory_space=pltpu.HBM)],
        out_specs=[vmem] * 4,
        scratch_shapes=[
            pltpu.VMEM((lead, lead), F),
            dma((row_tiles * tiles,)),
            dma((2 * tiles + 3 + 2 * row_tiles,)),
            dma((events, 4)),
            dma((events,)),
            dma((2, row_tiles, 2)),
            dma((2, row_tiles)),
            dma((4, 10)),
            dma((4,)),
        ],
        compiler_params=pltpu.CompilerParams(
            collective_id=0, has_side_effects=True, vmem_limit_bytes=24 * 2**20
        ),
        name="gather_and_factor",
    )(kernel_tiles)
    return pl.pallas_call(
        update_kernel,
        out_shape=jax.ShapeDtypeStruct(kernel_tiles.shape, F),
        in_specs=[vmem] * 4,
        out_specs=pl.BlockSpec(memory_space=pl.ANY),
        scratch_shapes=[
            pltpu.VMEM((lead, cols), BF),
            pltpu.VMEM((lead, cols), BF),
            pltpu.VMEM((2, nb, cols), F),
            dma((2, tiles)),
        ],
        compiler_params=pltpu.CompilerParams(vmem_limit_bytes=28 * 2**20),
        name="update",
    )(a, t, r, w)


def solution(mesh):
    spec = P(None, "prow", None, None, "pcol", None)
    return jax.shard_map(shards, mesh=mesh, in_specs=(spec,), out_specs=spec, check_vma=False)
```

```python
import functools

import jax
import jax.numpy as jnp
from jax import lax
from jax.experimental import pallas as pl
from jax.experimental.pallas import tpu as pltpu
from jax.sharding import PartitionSpec as P

MESH = pl.DeviceIdType.MESH
HI = lax.Precision.HIGHEST
F = jnp.float32
BF = jnp.bfloat16
NB = 256
SB = 128
SIDE = 4

TREE = {
    (0, 1): (1, 0), (3, 0): (-1, 0), (0, 3): (1, 0), (1, 0): (-1, 0), (0, 2): (1, 0),
    (2, 0): (-1, 0), (1, 1): (-1, 0), (3, 1): (0, 1), (3, 3): (0, -1), (1, 3): (-1, 0),
    (1, 2): (-1, 0), (2, 1): (0, 1), (3, 2): (0, -1), (2, 3): (-1, 0), (2, 2): (0, 1),
}
STEPS = ((1, 0), (-1, 0), (0, 1), (0, -1))
LAG = 2


def tree_parents():
    trees = [TREE]
    for _ in range(3):
        trees.append({((-x) % SIDE, z): (-s, d) for (z, x), (d, s) in trees[-1].items()})
    return trees


def children(tree, step):
    return [
        (v[0] - step[0]) % SIDE * SIDE + (v[1] - step[1]) % SIDE
        for v, d in tree.items()
        if d == step
    ]


def depths(tree):
    def depth(v):
        if v == (0, 0):
            return 0
        z, x = v
        d, s = tree[v]
        return 1 + depth(((z - d) % SIDE, (x - s) % SIDE))

    return [depth((v // SIDE, v % SIDE)) for v in range(SIDE * SIDE)]


def one_of(value, options):
    found = value == options[0]
    for other in options[1:]:
        found = found | (value == other)
    return found


def factor_block(x, after_leaf):
    n = x.shape[0]
    leaves = n // 8
    rows = [x[8 * i : 8 * i + 8] for i in range(leaves)]
    lane = lax.broadcasted_iota(jnp.int32, (8, n), 1)
    sub = lax.broadcasted_iota(jnp.int32, (8, n), 0)
    out = []
    for b in range(leaves):
        o = 8 * b
        c = [jnp.broadcast_to(rows[b][:, o + k : o + k + 1], (8, n)) for k in range(8)]
        inside = (lane >= o) & (lane < o + 8)
        g = jnp.where(inside, jnp.where(lane - o == sub, F(1), F(0)), rows[b])
        r = jnp.zeros_like(g)
        for j in range(8):
            pivot = jnp.broadcast_to(c[j][j : j + 1], (8, n))
            inv = 1.0 / pivot
            row = jnp.broadcast_to(g[j : j + 1], (8, n))
            here = sub == j
            r = jnp.where(here, row * lax.rsqrt(pivot), r)
            grow = row * inv
            g = jnp.where(here, grow, g - c[j] * grow)
            for k in range(j + 1, 8):
                ck = jnp.broadcast_to(c[k][j : j + 1], (8, n)) * inv
                c[k] = jnp.where(here, ck, c[k] - c[j] * ck)
        out.append(r)
        if b + 1 < leaves:
            below = rows[b + 1]
            acc = jnp.where(inside, F(0), below)
            for k in range(8):
                acc = acc - jnp.broadcast_to(below[:, o + k : o + k + 1], (8, n)) * jnp.broadcast_to(
                    g[k : k + 1], (8, n)
                )
            rows[b + 1] = acc
        if b + 2 < leaves:
            rest = jnp.concatenate(rows[b + 2 :], axis=0)
            parts = [g, jnp.zeros((n - o - 8, n), F)]
            if o:
                parts = [jnp.zeros((o, n), F)] + parts
            lanes = lax.broadcasted_iota(jnp.int32, rest.shape, 1)
            cleared = jnp.where((lanes >= o) & (lanes < o + 8), F(0), rest)
            rest = cleared - jnp.dot(rest, jnp.concatenate(parts, axis=0), precision=HI, preferred_element_type=F)
            for i in range(b + 2, leaves):
                rows[i] = rest[8 * (i - b - 2) : 8 * (i - b - 2) + 8]
        after_leaf()
    return jnp.concatenate(out, axis=0)


def factor_all(d_ref, w_ref, after_leaf, after_first):
    n = w_ref.shape[0]
    li = lax.broadcasted_iota(jnp.int32, (SB, SB), 1)
    si = lax.broadcasted_iota(jnp.int32, (SB, SB), 0)
    for r0 in range(0, n, SB):
        src = w_ref if r0 else d_ref
        here = pl.ds(r0, SB)
        f = factor_block(src[here, here], after_leaf)
        if not r0:
            after_first()
        w = jnp.where(li <= si, f, F(0))
        w_ref[here, :] = jnp.dot(w, src[here, :], precision=HI, preferred_element_type=F)
        w_ref[here, here] = w
        k0 = r0 + SB
        if k0 < n:
            rr = w_ref[here, :]
            upd = lax.dot_general(
                rr[:, k0:], rr, (((0,), (0,)), ((), ())), precision=HI, preferred_element_type=F
            )
            col = lax.broadcasted_iota(jnp.int32, (n - k0, n), 1)
            old = jnp.where((col >= r0) & (col < k0), F(0), src[pl.ds(k0, n - k0), :])
            w_ref[pl.ds(k0, n - k0), :] = old - upd
            w_ref[here, pl.ds(k0, n - k0)] = jnp.zeros((SB, n - k0), F)


def gather_kernel(
    x_ref, a_ref, t_ref, r_ref, w_ref, d_ref,
    sem_local, sem_stage, t_send, t_recv, top_send, top_recv, u_send, u_recv, r_send, r_recv, d_send, d_recv, w_send, w_recv,
):
    p = lax.axis_index("prow")
    q = lax.axis_index("pcol")
    z, x = p // SIDE, p % SIDE
    y, c = q // 2, q % 2
    tiles = x_ref.shape[3]
    row_tiles = x_ref.shape[0]
    first, second = c == 0, c == 1

    def dev(dz=0, dx=0, dy=0, other=False):
        cc = 1 - c if other else c
        return {
            "prow": (z + dz + SIDE) % SIDE * SIDE + (x + dx + SIDE) % SIDE,
            "pcol": (y + dy + SIDE) % SIDE * 2 + cc,
        }

    partner = dev(other=True)

    stage = []

    def bring(cond, src, dst):
        stage.append((cond, pltpu.make_async_copy(src, dst, sem_stage.at[len(stage)])))

    for row, col in ((0, 0), (0, 1), (1, 1)):
        bring(
            (p == row) & (q == col),
            x_ref.at[0, 0, :, 0, 0, :],
            d_ref.at[pl.ds(NB * row, NB), pl.ds(NB * col, NB)],
        )
    for k in range(2):
        for j in range(tiles):
            for slot in range(2):
                bring(
                    (p == k) & (c == slot),
                    x_ref.at[0, 0, :, j, 0, :],
                    t_ref.at[slot, pl.ds(NB * k, NB), pl.ds(NB * j, NB)],
                )
    for k in range(2):
        for i in range(row_tiles):
            bring(q == k, x_ref.at[i, 0, :, 0, 0, :], r_ref.at[k, pl.ds(NB * i, NB), :])
    for cond, copy in stage:
        pl.when(cond)(copy.start)
    own = [
        pltpu.make_async_copy(
            x_ref.at[i, 0, :, j, 0, :],
            a_ref.at[pl.ds(NB * i, NB), pl.ds(NB * j, NB)],
            sem_local.at[i * tiles + j],
        )
        for i in range(row_tiles)
        for j in range(tiles)
    ]
    for copy in own:
        copy.start()

    barrier = pltpu.get_barrier_semaphore()
    peers = [partner]
    for s in range(1, SIDE):
        peers += [dev(dz=s), dev(dx=s), dev(dy=s)]
    for peer in peers:
        pl.semaphore_signal(barrier, inc=1, device_id=peer, device_id_type=MESH)
    pl.semaphore_wait(barrier, len(peers))
    for cond, copy in stage:
        pl.when(cond)(copy.wait)

    sends = []

    def remote(src, dst, send, recv, peer):
        return pltpu.make_async_remote_copy(
            src_ref=src, dst_ref=dst, send_sem=send, recv_sem=recv, device_id=peer, device_id_type=MESH
        )

    def send(cond, copy):
        pl.when(cond)(copy.start)
        sends.append((cond, copy))

    pieces = [
        (0, 128, 0, 128, 0, 0),
        (0, 256, 128, 256, 0, 0),
        (0, 256, 256, 512, 0, 1),
        (256, 512, 256, 512, 1, 1),
    ]

    def line(s, direct):
        return ((s == 0, 1), (s == 0, 3), (s == 0 if direct else s == 1, 2 if direct else 1))

    def piece_ref(i):
        ra, rb, ca, cb, _, _ = pieces[i]
        return d_ref.at[pl.ds(ra, rb - ra), pl.ds(ca, cb - ca)]

    def hand_over(i):
        root = first & (z == 0) & (x == pieces[i][4]) & (y == 0)
        ref = piece_ref(i)
        send(root, remote(ref, ref, d_send.at[i, 9], d_recv.at[i], partner))

    def lead_piece(i):
        x0, c0 = pieces[i][4:]
        ref = piece_ref(i)
        rx = (x - x0 + SIDE) % SIDE
        source = second & (z == 0) & (rx == 0) & (y == 0)

        @pl.when(second if c0 == 0 else second & jnp.logical_not(source))
        def _():
            remote(ref, ref, d_send.at[i, 0], d_recv.at[i], partner).wait_recv()

        direct = i == 0
        for j, (cond, step) in enumerate(line(y, direct)):
            send(second & (z == 0) & (rx == 0) & cond, remote(ref, ref, d_send.at[i, j], d_recv.at[i], dev(dy=step)))
        for j, (cond, step) in enumerate(line(z, direct)):
            send(second & (rx == 0) & cond, remote(ref, ref, d_send.at[i, 3 + j], d_recv.at[i], dev(dz=step)))
        for j, (cond, step) in enumerate(line(rx, direct)):
            send(second & cond, remote(ref, ref, d_send.at[i, 6 + j], d_recv.at[i], dev(dx=step)))

    def row_chain(k, i):
        down = i >= row_tiles // 2
        step = SIDE - 1 if down else 1
        ref = r_ref.at[k, pl.ds(NB * i, NB), :]
        mine = c == k
        last = 1 if down else SIDE - 1

        @pl.when(mine & (y != 0))
        def _():
            remote(ref, ref, r_send.at[k, i, 0], r_recv.at[k, i], dev(dy=step)).wait_recv()

        send(mine & (y != last), remote(ref, ref, r_send.at[k, i, 0], r_recv.at[k, i], dev(dy=step)))
        send(mine, remote(ref, ref, r_send.at[k, i, 1], r_recv.at[k, i], partner))

    def row_partner(i):
        for k in range(2):
            ref = r_ref.at[k, pl.ds(NB * i, NB), :]

            @pl.when(c != k)
            def _():
                remote(ref, ref, r_send.at[k, i, 1], r_recv.at[k, i], partner).wait_recv()

    order = [row_tiles // 2, 0, row_tiles // 2 + 1, 1]

    trees = tree_parents()
    rel = [z * SIDE + (x - k + SIDE) % SIDE for k in range(2)]
    has = [[[one_of(rel[k], children(t, s)) for s in STEPS] for t in trees] for k in range(2)]
    deep = [depths(t) for t in trees]
    depth = [
        [sum(jnp.where(rel[k] == v, d, 0) for v, d in enumerate(deep[t])) for t in range(len(trees))]
        for k in range(2)
    ]
    most = max(max(d) for d in deep)
    share = NB // len(trees)
    count = share // 8 * 2
    peer4 = [dev(dz=dz, dx=dx) for dz, dx in STEPS]

    def chunk(k, t, i):
        start = pl.multiple_of(NB * k + share * t + i // 2 * 8, 8)
        return lambda slot: t_ref.at[slot, pl.ds(start, 8), :]

    def hop(k, t, i, j):
        e = k * len(trees) + t
        ref = chunk(k, t, i)(i % 2)
        return remote(ref, ref, t_send.at[e, i, j], t_recv.at[e, i], peer4[j])

    def over(k, t, i):
        e = k * len(trees) + t
        ref = chunk(k, t, i)
        return remote(ref(1), ref(0), u_send.at[e, i], u_recv.at[e], partner)

    def each(s, action):
        for k in range(2):
            for t in range(len(trees)):
                i = s - LAG * depth[k][t]

                @pl.when((i >= 0) & (i < count))
                def _():
                    action(k, t, i)

    def forward(k, t, i):
        @pl.when(depth[k][t] != 0)
        def _():
            hop(k, t, i, 0).wait_recv()

        for j in range(len(STEPS)):
            pl.when(has[k][t][j])(hop(k, t, i, j).start)
        pl.when(i % 2 == 1)(over(k, t, i).start)

    def sent(k, t, i):
        for j in range(len(STEPS)):
            pl.when(has[k][t][j])(hop(k, t, i, j).wait_send)
        pl.when(i % 2 == 1)(over(k, t, i).wait_send)

    steps = count + LAG * most

    def wave(lo, hi):
        def body(s, carry):
            each(s, forward)
            each(s - 8, sent)
            return carry

        lax.fori_loop(lo, hi, body, 0)

    tops = [
        remote(t_ref.at[1, pl.ds(NB * k, NB), :], t_ref.at[1, pl.ds(NB * k, NB), :], top_send.at[k], top_recv.at[k], partner)
        for k in range(2)
    ]
    for i in range(2):
        hand_over(i)
    for k in range(2):
        send(second & (p == k), tops[k])

    for i in range(len(pieces) if False else 1):
        lead_piece(i)

    todo = [functools.partial(lead_piece, i) for i in range(1, len(pieces))]
    todo += [functools.partial(row_chain, 1, i) for i in order]

    def after_leaf():
        if todo:
            todo.pop(0)()

    @pl.when(first)
    def _():
        for k in range(2):
            pl.when(p == k)(tops[k].wait_recv)
        wave(0, 4)

    row_chain(0, order[0])
    row_chain(0, order[1])

    @pl.when(first)
    def _():
        wave(4, 8)

    row_chain(0, order[2])
    row_chain(0, order[3])

    @pl.when(first)
    def _():
        wave(8, steps + 8)

    for item in todo:
        item()

    @pl.when(second)
    def _():
        factor_all(d_ref, w_ref, lambda: None, lambda: None)

    send(second, remote(w_ref, w_ref, w_send.at[0], w_recv.at[0], partner))

    @pl.when(first)
    def _():
        remote(w_ref, w_ref, w_send.at[0], w_recv.at[0], partner).wait_recv()

    @pl.when(second)
    def _():
        for k in range(2):
            for t in range(len(trees)):
                ref = t_ref.at[0, pl.ds(NB * k + share * t, share), :]
                remote(ref, ref, u_send.at[0, 0], u_recv.at[k * len(trees) + t], partner).wait_recv()

    for i in order:
        row_partner(i)
    for cond, copy in sends:
        pl.when(cond)(copy.wait_send)
    for copy in own:
        copy.wait()


def split(v):
    hi = v.astype(BF)
    return hi, (v - hi.astype(F)).astype(BF)


def dot(a, b):
    return jnp.dot(a, b, preferred_element_type=F)


def update_kernel(a_ref, t_ref, r_ref, w_ref, o_ref, thi, tlo, buf, sem):
    p = lax.axis_index("prow")
    q = lax.axis_index("pcol")
    prows = lax.axis_size("prow")
    tiles = a_ref.shape[1] // NB
    row_tiles = a_ref.shape[0] // NB
    ri = lax.broadcasted_iota(jnp.int32, (NB, NB), 0)
    ci = lax.broadcasted_iota(jnp.int32, (NB, NB), 1)
    for j in range(tiles):
        sl = pl.ds(NB * j, NB)
        hi, lo = split(t_ref[0, :, sl])
        thi[:, sl] = hi
        tlo[:, sl] = lo

    def copies(i, j):
        return pltpu.make_async_copy(
            buf.at[i % 2, :, pl.ds(NB * j, NB)], o_ref.at[i, 0, :, j, 0, :], sem.at[i % 2, j]
        )

    def body(i, carry):
        rows = pl.ds(pl.multiple_of(i * NB, NB), NB)
        ar = jnp.concatenate([r_ref[0, rows, :], r_ref[1, rows, :]], axis=1)
        w = w_ref[...]
        pr = lax.dot_general(ar, w, (((1,), (1,)), ((), ())), precision=HI, preferred_element_type=F)
        bhi, blo = split(jnp.dot(pr, w, precision=HI, preferred_element_type=F))
        row = i * prows + p
        active = row > 1

        @pl.when(i >= 2)
        def _():
            for j in range(tiles):
                copies(i - 2, j).wait()

        for j in range(tiles):
            sl = pl.ds(NB * j, NB)
            hi, lo = thi[:, sl], tlo[:, sl]
            val = a_ref[rows, sl] - (dot(bhi, hi) + (dot(bhi, lo) + dot(blo, hi)))
            val = jnp.where(active, val, F(0))
            if j == 0:
                panel = jnp.where(q == 0, pr[:, :NB], pr[:, NB:])
                keep = (row > q) | ((row == q) & (ci <= ri))
                val = jnp.where(q < 2, jnp.where(keep, panel, F(0)), val)
            buf[i % 2, :, sl] = val
            copies(i, j).start()
        return carry

    lax.fori_loop(0, row_tiles, body, 0)
    for i in range(row_tiles - 2, row_tiles):
        for j in range(tiles):
            copies(i, j).wait()


def shards(kernel_tiles):
    row_tiles, _, nb, tiles, _, _ = kernel_tiles.shape
    rows, cols, lead = row_tiles * nb, tiles * nb, 2 * nb
    vmem = pl.BlockSpec(memory_space=pltpu.VMEM)
    dma = pltpu.SemaphoreType.DMA
    count = nb // 4 // 8 * 2
    a, t, r, w = pl.pallas_call(
        gather_kernel,
        out_shape=[
            jax.ShapeDtypeStruct((rows, cols), F),
            jax.ShapeDtypeStruct((2, lead, cols), F),
            jax.ShapeDtypeStruct((2, rows, nb), F),
            jax.ShapeDtypeStruct((lead, lead), F),
        ],
        in_specs=[pl.BlockSpec(memory_space=pltpu.HBM)],
        out_specs=[vmem] * 4,
        scratch_shapes=[
            pltpu.VMEM((lead, lead), F),
            dma((row_tiles * tiles,)),
            dma((4 * tiles + 3 + 2 * row_tiles,)),
            dma((8, count, 4)),
            dma((8, count)),
            dma((2,)),
            dma((2,)),
            dma((8, count)),
            dma((8,)),
            dma((2, row_tiles, 2)),
            dma((2, row_tiles)),
            dma((4, 10)),
            dma((4,)),
            dma((1,)),
            dma((1,)),
        ],
        compiler_params=pltpu.CompilerParams(
            collective_id=0, has_side_effects=True, vmem_limit_bytes=44 * 2**20
        ),
        name="gather_and_factor",
    )(kernel_tiles)
    return pl.pallas_call(
        update_kernel,
        out_shape=jax.ShapeDtypeStruct(kernel_tiles.shape, F),
        in_specs=[vmem] * 4,
        out_specs=pl.BlockSpec(memory_space=pl.ANY),
        scratch_shapes=[
            pltpu.VMEM((lead, cols), BF),
            pltpu.VMEM((lead, cols), BF),
            pltpu.VMEM((2, nb, cols), F),
            dma((2, tiles)),
        ],
        compiler_params=pltpu.CompilerParams(vmem_limit_bytes=28 * 2**20),
        name="update",
    )(a, t, r, w)


def solution(mesh):
    spec = P(None, "prow", None, None, "pcol", None)
    return jax.shard_map(shards, mesh=mesh, in_specs=(spec,), out_specs=spec, check_vma=False)
```

```python
import functools

import jax
import jax.numpy as jnp
from jax import lax
from jax.experimental import pallas as pl
from jax.experimental.pallas import tpu as pltpu
from jax.sharding import PartitionSpec as P

MESH = pl.DeviceIdType.MESH
HI = lax.Precision.HIGHEST
F = jnp.float32
BF = jnp.bfloat16
NB = 256
SB = 128
SIDE = 4

TREE = {
    (0, 1): (1, 0), (3, 0): (-1, 0), (0, 3): (1, 0), (1, 0): (-1, 0), (0, 2): (1, 0),
    (2, 0): (-1, 0), (1, 1): (-1, 0), (3, 1): (0, 1), (3, 3): (0, -1), (1, 3): (-1, 0),
    (1, 2): (-1, 0), (2, 1): (0, 1), (3, 2): (0, -1), (2, 3): (-1, 0), (2, 2): (0, 1),
}
STEPS = ((1, 0), (-1, 0), (0, 1), (0, -1))
LAG = 3
LAG_LEAD = 3
LEAD = 7
ROW_CHUNKS = 4
ROW_START = 2
EVERY = 1
SPLIT = 1
PACE = 4


def tree_parents():
    trees = [TREE]
    for _ in range(3):
        trees.append({((-x) % SIDE, z): (-s, d) for (z, x), (d, s) in trees[-1].items()})
    return trees


def children(tree, step):
    return [
        (v[0] - step[0]) % SIDE * SIDE + (v[1] - step[1]) % SIDE
        for v, d in tree.items()
        if d == step
    ]


def depths(tree):
    def depth(v):
        if v == (0, 0):
            return 0
        z, x = v
        d, s = tree[v]
        return 1 + depth(((z - d) % SIDE, (x - s) % SIDE))

    return [depth((v // SIDE, v % SIDE)) for v in range(SIDE * SIDE)]


def one_of(value, options):
    found = value == options[0]
    for other in options[1:]:
        found = found | (value == other)
    return found


def factor_block(x, after_leaf):
    n = x.shape[0]
    leaves = n // 8
    rows = [x[8 * i : 8 * i + 8] for i in range(leaves)]
    lane = lax.broadcasted_iota(jnp.int32, (8, n), 1)
    sub = lax.broadcasted_iota(jnp.int32, (8, n), 0)
    out = []
    for b in range(leaves):
        o = 8 * b
        c = [jnp.broadcast_to(rows[b][:, o + k : o + k + 1], (8, n)) for k in range(8)]
        inside = (lane >= o) & (lane < o + 8)
        g = jnp.where(inside, jnp.where(lane - o == sub, F(1), F(0)), rows[b])
        r = jnp.zeros_like(g)
        for j in range(8):
            pivot = jnp.broadcast_to(c[j][j : j + 1], (8, n))
            inv = 1.0 / pivot
            row = jnp.broadcast_to(g[j : j + 1], (8, n))
            here = sub == j
            r = jnp.where(here, row * lax.rsqrt(pivot), r)
            grow = row * inv
            g = jnp.where(here, grow, g - c[j] * grow)
            for k in range(j + 1, 8):
                ck = jnp.broadcast_to(c[k][j : j + 1], (8, n)) * inv
                c[k] = jnp.where(here, ck, c[k] - c[j] * ck)
        out.append(r)
        if b + 1 < leaves:
            below = rows[b + 1]
            acc = jnp.where(inside, F(0), below)
            for k in range(8):
                acc = acc - jnp.broadcast_to(below[:, o + k : o + k + 1], (8, n)) * jnp.broadcast_to(
                    g[k : k + 1], (8, n)
                )
            rows[b + 1] = acc
        if b + 2 < leaves:
            rest = jnp.concatenate(rows[b + 2 :], axis=0)
            parts = [g, jnp.zeros((n - o - 8, n), F)]
            if o:
                parts = [jnp.zeros((o, n), F)] + parts
            lanes = lax.broadcasted_iota(jnp.int32, rest.shape, 1)
            cleared = jnp.where((lanes >= o) & (lanes < o + 8), F(0), rest)
            rest = cleared - jnp.dot(rest, jnp.concatenate(parts, axis=0), precision=HI, preferred_element_type=F)
            for i in range(b + 2, leaves):
                rows[i] = rest[8 * (i - b - 2) : 8 * (i - b - 2) + 8]
        after_leaf()
    return jnp.concatenate(out, axis=0)


def factor_all(d_ref, w_ref, after_leaf, after_first):
    n = w_ref.shape[0]
    li = lax.broadcasted_iota(jnp.int32, (SB, SB), 1)
    si = lax.broadcasted_iota(jnp.int32, (SB, SB), 0)
    for r0 in range(0, n, SB):
        src = w_ref if r0 else d_ref
        here = pl.ds(r0, SB)
        f = factor_block(src[here, here], after_leaf)
        if not r0:
            after_first()
        w = jnp.where(li <= si, f, F(0))
        w_ref[here, :] = jnp.dot(w, src[here, :], precision=HI, preferred_element_type=F)
        w_ref[here, here] = w
        k0 = r0 + SB
        if k0 < n:
            rr = w_ref[here, :]
            upd = lax.dot_general(
                rr[:, k0:], rr, (((0,), (0,)), ((), ())), precision=HI, preferred_element_type=F
            )
            col = lax.broadcasted_iota(jnp.int32, (n - k0, n), 1)
            old = jnp.where((col >= r0) & (col < k0), F(0), src[pl.ds(k0, n - k0), :])
            w_ref[pl.ds(k0, n - k0), :] = old - upd
            w_ref[here, pl.ds(k0, n - k0)] = jnp.zeros((SB, n - k0), F)


def gather_kernel(
    x_ref, a_ref, t_ref, r_ref, w_ref, d_ref,
    sem_local, sem_stage, t_send, t_recv, r_send, r_recv, s_send, s_recv, d_send, d_recv, h_send, h_recv,
):
    p = lax.axis_index("prow")
    q = lax.axis_index("pcol")
    z, x = p // SIDE, p % SIDE
    y, c = q // 2, q % 2
    tiles = x_ref.shape[3]
    row_tiles = x_ref.shape[0]

    def dev(dz=0, dx=0, dy=0, other=False):
        cc = 1 - c if other else c
        return {
            "prow": (z + dz + SIDE) % SIDE * SIDE + (x + dx + SIDE) % SIDE,
            "pcol": (y + dy + SIDE) % SIDE * 2 + cc,
        }

    partner = dev(other=True)

    stage = []

    def bring(cond, src, dst):
        stage.append((cond, pltpu.make_async_copy(src, dst, sem_stage.at[len(stage)])))

    for row, col in ((0, 0), (0, 1), (1, 1)):
        bring(
            (p == row) & (q == col),
            x_ref.at[0, 0, :, 0, 0, :],
            d_ref.at[pl.ds(NB * row, NB), pl.ds(NB * col, NB)],
        )
    for k in range(2):
        for j in range(tiles):
            bring(p == k, x_ref.at[0, 0, :, j, 0, :], t_ref.at[pl.ds(NB * k, NB), pl.ds(NB * j, NB)])
    for k in range(2):
        for i in range(row_tiles):
            bring(q == k, x_ref.at[i, 0, :, 0, 0, :], r_ref.at[k, pl.ds(NB * i, NB), :])
    for cond, copy in stage:
        pl.when(cond)(copy.start)
    own = [
        pltpu.make_async_copy(
            x_ref.at[i, 0, :, j, 0, :],
            a_ref.at[pl.ds(NB * i, NB), pl.ds(NB * j, NB)],
            sem_local.at[i * tiles + j],
        )
        for i in range(row_tiles)
        for j in range(tiles)
    ]

    barrier = pltpu.get_barrier_semaphore()
    peers = [partner]
    for s in range(1, SIDE):
        peers += [dev(dz=s), dev(dx=s), dev(dy=s)]
    for peer in peers:
        pl.semaphore_signal(barrier, inc=1, device_id=peer, device_id_type=MESH)
    pl.semaphore_wait(barrier, len(peers))
    for cond, copy in stage:
        pl.when(cond)(copy.wait)

    def remote(ref, send, recv, peer):
        return pltpu.make_async_remote_copy(
            src_ref=ref, dst_ref=ref, send_sem=send, recv_sem=recv, device_id=peer, device_id_type=MESH
        )

    sends = []

    def send(cond, copy):
        pl.when(cond)(copy.start)
        sends.append((cond, copy))

    pieces = [
        (0, 128, 0, 128, 0, 0, 0, 0),
        (0, 128, 128, 256, 0, 0, 0, 1),
        (0, 128, 256, 512, 0, 1, 1, 0),
        (128, 256, 128, 256, 0, 0, 0, 2),
        (128, 256, 256, 512, 0, 1, 1, 1),
        (256, 384, 256, 512, 1, 0, 1, 2),
        (384, 512, 384, 512, 1, 0, 1, 3),
    ]
    assert len(pieces) == LEAD

    def piece(i):
        ra, rb, ca, cb = pieces[i][:4]
        ref = d_ref.at[pl.ds(ra, rb - ra), pl.ds(ca, cb - ca)]
        return lambda j, peer: remote(ref, d_send.at[i, j], d_recv.at[i], peer)

    def handed(i):
        return pieces[i][5] != pieces[i][6]

    def root_chip(i):
        return (z == 0) & (x == pieces[i][4]) & (y == 0)

    def hand(i):
        if handed(i):
            send(root_chip(i) & (c == pieces[i][6]), piece(i)(9, partner))

    def lead(i, s):
        x0, c0, owner, begin = pieces[i][4:]
        copy = piece(i)
        mine = c == c0
        rx = (x - x0 + SIDE) % SIDE
        on_y = (z == 0) & (rx == 0)
        place = jnp.where(rx != 0, 3, jnp.where(z != 0, 2, jnp.where(y != 0, 1, 0)))
        k = s - begin - LAG_LEAD * place

        @pl.when(mine & (k == 0))
        def _():
            @pl.when(place != 0 if c0 == owner else place >= 0)
            def _():
                copy(0, partner).wait_recv()

            for step in range(1, SIDE):
                pl.when(on_y & (y == 0))(copy(step - 1, dev(dy=step)).start)
                pl.when((rx == 0) & (z == 0))(copy(step + 2, dev(dz=step)).start)
                pl.when(rx == 0)(copy(step + 5, dev(dx=step)).start)
            if c0 == owner:
                copy(9, partner).start()
            else:
                pl.when(place != 0)(copy(9, partner).start)

        @pl.when(jnp.logical_not(mine) & (k == 1))
        def _():
            pl.when((place != 0) if c0 != owner else (place >= 0))(copy(9, partner).wait_recv)

    def lead_sent(i):
        x0, c0, owner, _ = pieces[i][4:]
        copy = piece(i)
        mine = c == c0
        rx = (x - x0 + SIDE) % SIDE
        home = (z == 0) & (rx == 0) & (y == 0)

        @pl.when(mine)
        def _():
            for step in range(1, SIDE):
                pl.when(home)(copy(step - 1, dev(dy=step)).wait_send)
                pl.when((rx == 0) & (z == 0))(copy(step + 2, dev(dz=step)).wait_send)
                pl.when(rx == 0)(copy(step + 5, dev(dx=step)).wait_send)
            if c0 == owner:
                copy(9, partner).wait_send()
            else:
                pl.when(jnp.logical_not(home))(copy(9, partner).wait_send)

    half = row_tiles * NB // 2
    piece_rows = half // ROW_CHUNKS

    def row_copy(down, i, j, peer):
        ref = r_ref.at[c, pl.ds(pl.multiple_of(down * half + i * piece_rows, piece_rows), piece_rows), :]
        recv = s_recv.at[0] if j == 1 else r_recv.at[down, i]
        return remote(ref, (s_send if j == 1 else r_send).at[down, i], recv, peer)

    def row_each(s, action):
        for down in range(2):
            far = (SIDE - y) % SIDE if down else y
            since = s - ROW_START - LAG * far
            i = since // EVERY
            pl.when((since >= 0) & (since % EVERY == 0) & (i < ROW_CHUNKS))(functools.partial(action, down, i, far))

    def row_pass(down, i, far):
        peer = dev(dy=SIDE - 1 if down else 1)
        pl.when(far != 0)(row_copy(down, i, 0, peer).wait_recv)
        pl.when(far != SIDE - 1)(row_copy(down, i, 0, peer).start)
        row_copy(down, i, 1, partner).start()

    def row_sent(down, i, far):
        peer = dev(dy=SIDE - 1 if down else 1)
        pl.when(far != SIDE - 1)(row_copy(down, i, 0, peer).wait_send)
        row_copy(down, i, 1, partner).wait_send()

    trees = tree_parents()
    rel = [z * SIDE + (x - k + SIDE) % SIDE for k in range(2)]
    has = [[[one_of(rel[k], children(t, s)) for s in STEPS] for t in trees] for k in range(2)]
    deep = [depths(t) for t in trees]
    depth = [
        [sum(jnp.where(rel[k] == v, d, 0) for v, d in enumerate(deep[t])) for t in range(len(trees))]
        for k in range(2)
    ]
    most = max(max(d) for d in deep)
    share = NB // len(trees)
    count = share // 8 * SPLIT
    wide = t_ref.shape[1] // SPLIT
    peer4 = [dev(dz=dz, dx=dx) for dz, dx in STEPS]

    def hop(k, t, i, j):
        e = k * len(trees) + t
        start = pl.multiple_of(NB * k + share * t + i // SPLIT * 8, 8)
        ref = t_ref.at[pl.ds(start, 8), pl.ds(pl.multiple_of(i % SPLIT * wide, wide), wide)]
        return remote(ref, t_send.at[e, i, j], t_recv.at[e, i], peer4[j])

    def tree_each(s, action):
        for k in range(2):
            for t in range(len(trees)):
                since = s - k - LAG * depth[k][t]
                i = since // EVERY
                pl.when((since >= 0) & (since % EVERY == 0) & (i < count))(functools.partial(action, k, t, i))

    def forward(k, t, i):
        pl.when(depth[k][t] != 0)(hop(k, t, i, 0).wait_recv)
        for j in range(len(STEPS)):
            pl.when(has[k][t][j])(hop(k, t, i, j).start)

    def sent(k, t, i):
        for j in range(len(STEPS)):
            pl.when(has[k][t][j])(hop(k, t, i, j).wait_send)

    last_lead = max(v[7] for v in pieces) + 3 * LAG_LEAD + 1
    last_row = ROW_START + EVERY * (ROW_CHUNKS - 1) + LAG * (SIDE - 1)
    last_tree = EVERY * (count - 1) + LAG * most + 1
    steps = 1 + max(last_tree, last_lead, last_row)

    def wave(s):
        for i in range(len(pieces)):
            if not isinstance(s, int) or pieces[i][7] <= s <= pieces[i][7] + 3 * LAG_LEAD + 1:
                lead(i, s)
        if not isinstance(s, int) or s <= last_row:
            row_each(s, row_pass)
        tree_each(s, forward)

    for i in range(len(pieces)):
        hand(i)

    def early(s, carry):
        wave(s)
        return carry

    first_wave = 3 * LAG_LEAD + 2
    lax.fori_loop(0, 2, early, 0)
    for copy in own:
        copy.start()
    lax.fori_loop(2, first_wave, early, 0)
    later = list(range(first_wave, steps))
    leaf = [0]

    def after_leaf():
        leaf[0] += 1
        if leaf[0] % PACE == 0 and later:
            wave(later.pop(0))

    def after_first():
        while later and later[0] <= last_lead:
            wave(later.pop(0))

    factor_all(d_ref, w_ref, after_leaf, after_first)
    while later:
        wave(later.pop(0))
    ref = r_ref.at[1 - c]
    remote(ref, s_send.at[0, 0], s_recv.at[0], partner).wait_recv()

    def drain(s, carry):
        tree_each(s, sent)
        row_each(s, row_sent)
        return carry

    lax.fori_loop(0, steps, drain, 0)
    for i in range(len(pieces)):
        lead_sent(i)
    for cond, copy in sends:
        pl.when(cond)(copy.wait_send)
    for copy in own:
        copy.wait()


def split(v):
    hi = v.astype(BF)
    return hi, (v - hi.astype(F)).astype(BF)


def dot(a, b):
    return jnp.dot(a, b, preferred_element_type=F)


def exact(a, b, dims=(((1,), (0,)), ((), ()))):
    return lax.dot_general(a, b, dims, precision=HI, preferred_element_type=F)


def update_kernel(a_ref, t_ref, r_ref, w_ref, o_ref, pan, bhi, blo, buf, sem):
    p = lax.axis_index("prow")
    q = lax.axis_index("pcol")
    tiles = a_ref.shape[1] // NB
    row_tiles = a_ref.shape[0] // NB
    across = (((1,), (1,)), ((), ()))
    w00 = w_ref[:NB, :NB]
    w1 = w_ref[NB:, :]
    w11 = w_ref[NB:, NB:]
    r0, r1 = r_ref[0], r_ref[1]
    pan[0] = exact(r0, w00, across)
    pan[1] = exact(r0, w1[:, :NB], across) + exact(r1, w11, across)
    for k, v in ((0, exact(pan[0], w00) + exact(pan[1], w1[:, :NB])), (1, exact(pan[1], w11))):
        hi, lo = split(v)
        bhi[:, NB * k : NB * k + NB] = hi
        blo[:, NB * k : NB * k + NB] = lo

    def copy(j, i):
        return pltpu.make_async_copy(
            buf.at[j % 2, pl.ds(NB * i, NB), :], o_ref.at[i, 0, :, j, 0, :], sem.at[j % 2, i]
        )

    def body(j, carry):
        sl = pl.ds(pl.multiple_of(j * NB, NB), NB)
        hi, lo = split(t_ref[:, sl])

        @pl.when(j >= 2)
        def _():
            for i in range(row_tiles):
                copy(j - 2, i).wait()

        for i in range(row_tiles):
            rows = slice(NB * i, NB * i + NB)
            h, l = bhi[rows, :], blo[rows, :]
            buf[j % 2, rows, :] = a_ref[rows, sl] - (dot(h, hi) + (dot(h, lo) + dot(l, hi)))

        @pl.when(p <= 1)
        def _():
            buf[j % 2, :NB, :] = jnp.zeros((NB, NB), F)

        for k in range(2):

            @pl.when((j == 0) & (q == k))
            def _():
                buf[0] = pan[k]
                ri = lax.broadcasted_iota(jnp.int32, (NB, NB), 0)
                ci = lax.broadcasted_iota(jnp.int32, (NB, NB), 1)
                keep = (p > k) | ((p == k) & (ci <= ri))
                buf[0, :NB, :] = jnp.where(keep, pan[k, :NB, :], F(0))

        for i in range(row_tiles):
            copy(j, i).start()
        return carry

    lax.fori_loop(0, tiles, body, 0)
    for j in range(tiles - 2, tiles):
        for i in range(row_tiles):
            copy(j, i).wait()


def shards(kernel_tiles):
    row_tiles, _, nb, tiles, _, _ = kernel_tiles.shape
    rows, cols, lead = row_tiles * nb, tiles * nb, 2 * nb
    vmem = pl.BlockSpec(memory_space=pltpu.VMEM)
    dma = pltpu.SemaphoreType.DMA
    count = nb // 4 // 8 * SPLIT
    a, t, r, w = pl.pallas_call(
        gather_kernel,
        out_shape=[
            jax.ShapeDtypeStruct((rows, cols), F),
            jax.ShapeDtypeStruct((lead, cols), F),
            jax.ShapeDtypeStruct((2, rows, nb), F),
            jax.ShapeDtypeStruct((lead, lead), F),
        ],
        in_specs=[pl.BlockSpec(memory_space=pltpu.HBM)],
        out_specs=[vmem] * 4,
        scratch_shapes=[
            pltpu.VMEM((lead, lead), F),
            dma((row_tiles * tiles,)),
            dma((2 * tiles + 3 + 2 * row_tiles,)),
            dma((8, count, 4)),
            dma((8, count)),
            dma((2, ROW_CHUNKS)),
            dma((2, ROW_CHUNKS)),
            dma((2, ROW_CHUNKS)),
            dma((1,)),
            dma((LEAD, 10)),
            dma((LEAD,)),
            dma((1,)),
            dma((1,)),
        ],
        compiler_params=pltpu.CompilerParams(
            collective_id=0, has_side_effects=True, vmem_limit_bytes=32 * 2**20
        ),
        name="gather_and_factor",
    )(kernel_tiles)
    return pl.pallas_call(
        update_kernel,
        out_shape=jax.ShapeDtypeStruct(kernel_tiles.shape, F),
        in_specs=[vmem] * 4,
        out_specs=pl.BlockSpec(memory_space=pl.ANY),
        scratch_shapes=[
            pltpu.VMEM((2, rows, nb), F),
            pltpu.VMEM((rows, lead), BF),
            pltpu.VMEM((rows, lead), BF),
            pltpu.VMEM((2, rows, nb), F),
            dma((2, row_tiles)),
        ],
        compiler_params=pltpu.CompilerParams(vmem_limit_bytes=28 * 2**20),
        name="update",
    )(a, t, r, w)


def solution(mesh):
    spec = P(None, "prow", None, None, "pcol", None)
    return jax.shard_map(shards, mesh=mesh, in_specs=(spec,), out_specs=spec, check_vma=False)
```

```python
import functools

import jax
import jax.numpy as jnp
from jax import lax
from jax.experimental import pallas as pl
from jax.experimental.pallas import tpu as pltpu
from jax.sharding import PartitionSpec as P

MESH = pl.DeviceIdType.MESH
HI = lax.Precision.HIGHEST
F = jnp.float32
BF = jnp.bfloat16
NB = 256
SB = 128
SIDE = 4

TREE = {
    (0, 1): (1, 0), (3, 0): (-1, 0), (0, 3): (1, 0), (1, 0): (-1, 0), (0, 2): (1, 0),
    (2, 0): (-1, 0), (1, 1): (-1, 0), (3, 1): (0, 1), (3, 3): (0, -1), (1, 3): (-1, 0),
    (1, 2): (-1, 0), (2, 1): (0, 1), (3, 2): (0, -1), (2, 3): (-1, 0), (2, 2): (0, 1),
}
STEPS = ((1, 0), (-1, 0), (0, 1), (0, -1))
LAG = 3
LAG_LEAD = 3
LEAD = 7
ROW_CHUNKS = 4
ROW_START = 2
TREE_START = 5
PACE = 4


def tree_parents():
    trees = [TREE]
    for _ in range(3):
        trees.append({((-x) % SIDE, z): (-s, d) for (z, x), (d, s) in trees[-1].items()})
    return trees


def children(tree, step):
    return [
        (v[0] - step[0]) % SIDE * SIDE + (v[1] - step[1]) % SIDE
        for v, d in tree.items()
        if d == step
    ]


def depths(tree):
    def depth(v):
        if v == (0, 0):
            return 0
        z, x = v
        d, s = tree[v]
        return 1 + depth(((z - d) % SIDE, (x - s) % SIDE))

    return [depth((v // SIDE, v % SIDE)) for v in range(SIDE * SIDE)]


def one_of(value, options):
    found = value == options[0]
    for other in options[1:]:
        found = found | (value == other)
    return found


def factor_block(x, after_leaf):
    n = x.shape[0]
    leaves = n // 8
    rows = [x[8 * i : 8 * i + 8] for i in range(leaves)]
    lane = lax.broadcasted_iota(jnp.int32, (8, n), 1)
    sub = lax.broadcasted_iota(jnp.int32, (8, n), 0)
    out = []
    for b in range(leaves):
        o = 8 * b
        c = [jnp.broadcast_to(rows[b][:, o + k : o + k + 1], (8, n)) for k in range(8)]
        inside = (lane >= o) & (lane < o + 8)
        g = jnp.where(inside, jnp.where(lane - o == sub, F(1), F(0)), rows[b])
        r = jnp.zeros_like(g)
        for j in range(8):
            pivot = jnp.broadcast_to(c[j][j : j + 1], (8, n))
            inv = 1.0 / pivot
            row = jnp.broadcast_to(g[j : j + 1], (8, n))
            here = sub == j
            r = jnp.where(here, row * lax.rsqrt(pivot), r)
            grow = row * inv
            g = jnp.where(here, grow, g - c[j] * grow)
            for k in range(j + 1, 8):
                ck = jnp.broadcast_to(c[k][j : j + 1], (8, n)) * inv
                c[k] = jnp.where(here, ck, c[k] - c[j] * ck)
        out.append(r)
        if b + 1 < leaves:
            below = rows[b + 1]
            acc = jnp.where(inside, F(0), below)
            for k in range(8):
                acc = acc - jnp.broadcast_to(below[:, o + k : o + k + 1], (8, n)) * jnp.broadcast_to(
                    g[k : k + 1], (8, n)
                )
            rows[b + 1] = acc
        if b + 2 < leaves:
            rest = jnp.concatenate(rows[b + 2 :], axis=0)
            parts = [g, jnp.zeros((n - o - 8, n), F)]
            if o:
                parts = [jnp.zeros((o, n), F)] + parts
            lanes = lax.broadcasted_iota(jnp.int32, rest.shape, 1)
            cleared = jnp.where((lanes >= o) & (lanes < o + 8), F(0), rest)
            rest = cleared - jnp.dot(rest, jnp.concatenate(parts, axis=0), precision=HI, preferred_element_type=F)
            for i in range(b + 2, leaves):
                rows[i] = rest[8 * (i - b - 2) : 8 * (i - b - 2) + 8]
        after_leaf()
    return jnp.concatenate(out, axis=0)


def factor_all(d_ref, w_ref, after_leaf, after_first):
    n = w_ref.shape[0]
    li = lax.broadcasted_iota(jnp.int32, (SB, SB), 1)
    si = lax.broadcasted_iota(jnp.int32, (SB, SB), 0)
    for r0 in range(0, n, SB):
        src = w_ref if r0 else d_ref
        here = pl.ds(r0, SB)
        f = factor_block(src[here, here], after_leaf)
        if not r0:
            after_first()
        w = jnp.where(li <= si, f, F(0))
        w_ref[here, :] = jnp.dot(w, src[here, :], precision=HI, preferred_element_type=F)
        w_ref[here, here] = w
        k0 = r0 + SB
        if k0 < n:
            rr = w_ref[here, :]
            upd = lax.dot_general(
                rr[:, k0:], rr, (((0,), (0,)), ((), ())), precision=HI, preferred_element_type=F
            )
            col = lax.broadcasted_iota(jnp.int32, (n - k0, n), 1)
            old = jnp.where((col >= r0) & (col < k0), F(0), src[pl.ds(k0, n - k0), :])
            w_ref[pl.ds(k0, n - k0), :] = old - upd
            w_ref[here, pl.ds(k0, n - k0)] = jnp.zeros((SB, n - k0), F)


def gather_kernel(
    x_ref, a_ref, t_ref, r_ref, w_ref, d_ref,
    sem_local, sem_stage, t_send, t_recv, r_send, r_recv, s_send, s_recv, d_send, d_recv, h_send, h_recv,
):
    p = lax.axis_index("prow")
    q = lax.axis_index("pcol")
    z, x = p // SIDE, p % SIDE
    y, c = q // 2, q % 2
    tiles = x_ref.shape[3]
    row_tiles = x_ref.shape[0]

    def dev(dz=0, dx=0, dy=0, other=False):
        cc = 1 - c if other else c
        return {
            "prow": (z + dz + SIDE) % SIDE * SIDE + (x + dx + SIDE) % SIDE,
            "pcol": (y + dy + SIDE) % SIDE * 2 + cc,
        }

    partner = dev(other=True)

    stage = []

    def bring(cond, src, dst):
        stage.append((cond, pltpu.make_async_copy(src, dst, sem_stage.at[len(stage)])))

    for row, col in ((0, 0), (0, 1), (1, 1)):
        bring(
            (p == row) & (q == col),
            x_ref.at[0, 0, :, 0, 0, :],
            d_ref.at[pl.ds(NB * row, NB), pl.ds(NB * col, NB)],
        )
    for k in range(2):
        for j in range(tiles):
            bring(p == k, x_ref.at[0, 0, :, j, 0, :], t_ref.at[pl.ds(NB * k, NB), pl.ds(NB * j, NB)])
    for k in range(2):
        for i in range(row_tiles):
            bring(q == k, x_ref.at[i, 0, :, 0, 0, :], r_ref.at[k, pl.ds(NB * i, NB), :])
    for cond, copy in stage:
        pl.when(cond)(copy.start)
    own = [
        pltpu.make_async_copy(
            x_ref.at[i, 0, :, j, 0, :],
            a_ref.at[pl.ds(NB * i, NB), pl.ds(NB * j, NB)],
            sem_local.at[i * tiles + j],
        )
        for i in range(row_tiles)
        for j in range(tiles)
    ]

    barrier = pltpu.get_barrier_semaphore()
    peers = [partner]
    for s in range(1, SIDE):
        peers += [dev(dz=s), dev(dx=s), dev(dy=s)]
    for peer in peers:
        pl.semaphore_signal(barrier, inc=1, device_id=peer, device_id_type=MESH)
    pl.semaphore_wait(barrier, len(peers))
    for cond, copy in stage:
        pl.when(cond)(copy.wait)

    def remote(ref, send, recv, peer):
        return pltpu.make_async_remote_copy(
            src_ref=ref, dst_ref=ref, send_sem=send, recv_sem=recv, device_id=peer, device_id_type=MESH
        )

    sends = []

    def send(cond, copy):
        pl.when(cond)(copy.start)
        sends.append((cond, copy))

    pieces = [
        (0, 128, 0, 128, 0, 0, 0, 0),
        (0, 128, 128, 256, 0, 0, 0, 1),
        (0, 128, 256, 512, 0, 1, 1, 0),
        (128, 256, 128, 256, 0, 0, 0, 2),
        (128, 256, 256, 512, 0, 1, 1, 1),
        (256, 384, 256, 512, 1, 0, 1, 2),
        (384, 512, 384, 512, 1, 0, 1, 3),
    ]
    assert len(pieces) == LEAD

    def piece(i):
        ra, rb, ca, cb = pieces[i][:4]
        ref = d_ref.at[pl.ds(ra, rb - ra), pl.ds(ca, cb - ca)]
        return lambda j, peer: remote(ref, d_send.at[i, j], d_recv.at[i], peer)

    def handed(i):
        return pieces[i][5] != pieces[i][6]

    def root_chip(i):
        return (z == 0) & (x == pieces[i][4]) & (y == 0)

    def hand(i):
        if handed(i):
            send(root_chip(i) & (c == pieces[i][6]), piece(i)(9, partner))

    def lead(i, s):
        x0, c0, owner, begin = pieces[i][4:]
        copy = piece(i)
        mine = c == c0
        rx = (x - x0 + SIDE) % SIDE
        on_y = (z == 0) & (rx == 0)
        place = jnp.where(rx != 0, 3, jnp.where(z != 0, 2, jnp.where(y != 0, 1, 0)))
        k = s - begin - LAG_LEAD * place

        @pl.when(mine & (k == 0))
        def _():
            @pl.when(place != 0 if c0 == owner else place >= 0)
            def _():
                copy(0, partner).wait_recv()

            for step in range(1, SIDE):
                pl.when(on_y & (y == 0))(copy(step - 1, dev(dy=step)).start)
                pl.when((rx == 0) & (z == 0))(copy(step + 2, dev(dz=step)).start)
                pl.when(rx == 0)(copy(step + 5, dev(dx=step)).start)
            if c0 == owner:
                copy(9, partner).start()
            else:
                pl.when(place != 0)(copy(9, partner).start)

        @pl.when(jnp.logical_not(mine) & (k == 1))
        def _():
            pl.when((place != 0) if c0 != owner else (place >= 0))(copy(9, partner).wait_recv)

    def lead_sent(i):
        x0, c0, owner, _ = pieces[i][4:]
        copy = piece(i)
        mine = c == c0
        rx = (x - x0 + SIDE) % SIDE
        home = (z == 0) & (rx == 0) & (y == 0)

        @pl.when(mine)
        def _():
            for step in range(1, SIDE):
                pl.when(home)(copy(step - 1, dev(dy=step)).wait_send)
                pl.when((rx == 0) & (z == 0))(copy(step + 2, dev(dz=step)).wait_send)
                pl.when(rx == 0)(copy(step + 5, dev(dx=step)).wait_send)
            if c0 == owner:
                copy(9, partner).wait_send()
            else:
                pl.when(jnp.logical_not(home))(copy(9, partner).wait_send)

    half = row_tiles * NB // 2
    piece_rows = half // ROW_CHUNKS

    def row_copy(down, i, j, peer):
        ref = r_ref.at[c, pl.ds(pl.multiple_of(down * half + i * piece_rows, piece_rows), piece_rows), :]
        recv = s_recv.at[0] if j == 1 else r_recv.at[down, i]
        return remote(ref, (s_send if j == 1 else r_send).at[down], recv, peer)

    def row_each(s, action):
        for down in range(2):
            far = (SIDE - y) % SIDE if down else y
            i = s - ROW_START - LAG * far
            pl.when((i >= 0) & (i < ROW_CHUNKS))(functools.partial(action, down, i, far))

    def row_pass(down, i, far):
        peer = dev(dy=SIDE - 1 if down else 1)
        pl.when(far != 0)(row_copy(down, i, 0, peer).wait_recv)
        pl.when(far != SIDE - 1)(row_copy(down, i, 0, peer).start)
        row_copy(down, i, 1, partner).start()

    def rows_sent():
        for down in range(2):
            far = (SIDE - y) % SIDE if down else y
            ref = r_ref.at[c, pl.ds(down * half, half), :]
            pl.when(far != SIDE - 1)(remote(ref, r_send.at[down], r_recv.at[down, 0], partner).wait_send)
            remote(ref, s_send.at[down], s_recv.at[0], partner).wait_send()

    trees = tree_parents()
    rel = [z * SIDE + (x - k + SIDE) % SIDE for k in range(2)]
    has = [[[one_of(rel[k], children(t, s)) for s in STEPS] for t in trees] for k in range(2)]
    deep = [depths(t) for t in trees]
    depth = [
        [sum(jnp.where(rel[k] == v, d, 0) for v, d in enumerate(deep[t])) for t in range(len(trees))]
        for k in range(2)
    ]
    most = max(max(d) for d in deep)
    share = NB // len(trees)
    count = share // 8
    begin = [[TREE_START + LAG * d for d in row] for row in depth]
    peer4 = [dev(dz=dz, dx=dx) for dz, dx in STEPS]

    def hop(k, t, i, j):
        e = k * len(trees) + t
        ref = t_ref.at[pl.ds(pl.multiple_of(NB * k + share * t + i * 8, 8), 8), :]
        return remote(ref, t_send.at[e, j], t_recv.at[e, i], peer4[j])

    def tree_each(s, action):
        for k in range(2):
            for t in range(len(trees)):
                i = s - begin[k][t]
                pl.when((i >= 0) & (i < count))(functools.partial(action, k, t, i))

    def forward(k, t, i):
        pl.when(depth[k][t] != 0)(hop(k, t, i, 0).wait_recv)
        for j in range(len(STEPS)):
            pl.when(has[k][t][j])(hop(k, t, i, j).start)

    def trees_sent():
        for k in range(2):
            for t in range(len(trees)):
                e = k * len(trees) + t
                ref = t_ref.at[pl.ds(NB * k + share * t, share), :]
                for j in range(len(STEPS)):
                    pl.when(has[k][t][j])(remote(ref, t_send.at[e, j], t_recv.at[e, 0], peer4[j]).wait_send)

    last_lead = max(v[7] for v in pieces) + 3 * LAG_LEAD + 1
    last_row = ROW_START + ROW_CHUNKS - 1 + LAG * (SIDE - 1)
    last_tree = TREE_START + count - 1 + LAG * most
    steps = 1 + max(last_tree, last_lead, last_row)

    def wave(s):
        for i in range(len(pieces)):
            if not isinstance(s, int) or pieces[i][7] <= s <= pieces[i][7] + 3 * LAG_LEAD + 1:
                lead(i, s)
        if not isinstance(s, int) or s <= last_row:
            row_each(s, row_pass)
        tree_each(s, forward)

    for i in range(len(pieces)):
        hand(i)

    def early(s, carry):
        wave(s)
        return carry

    first_wave = 3 * LAG_LEAD + 2
    lax.fori_loop(0, 2, early, 0)
    for copy in own:
        copy.start()
    lax.fori_loop(2, first_wave, early, 0)
    later = list(range(first_wave, steps))
    leaf = [0]

    def after_leaf():
        leaf[0] += 1
        if leaf[0] % PACE == 0 and later:
            wave(later.pop(0))

    def after_first():
        while later and later[0] <= last_lead:
            wave(later.pop(0))

    factor_all(d_ref, w_ref, after_leaf, after_first)
    while later:
        wave(later.pop(0))
    ref = r_ref.at[1 - c]
    remote(ref, s_send.at[0], s_recv.at[0], partner).wait_recv()

    trees_sent()
    rows_sent()
    for i in range(len(pieces)):
        lead_sent(i)
    for cond, copy in sends:
        pl.when(cond)(copy.wait_send)
    for copy in own:
        copy.wait()


def split(v):
    hi = v.astype(BF)
    return hi, (v - hi.astype(F)).astype(BF)


def dot(a, b):
    return jnp.dot(a, b, preferred_element_type=F)


def exact(a, b, dims=(((1,), (0,)), ((), ()))):
    return lax.dot_general(a, b, dims, precision=HI, preferred_element_type=F)


def update_kernel(a_ref, t_ref, r_ref, w_ref, o_ref, pan, bhi, blo, buf, sem):
    p = lax.axis_index("prow")
    q = lax.axis_index("pcol")
    tiles = a_ref.shape[1] // NB
    row_tiles = a_ref.shape[0] // NB
    across = (((1,), (1,)), ((), ()))
    w00 = w_ref[:NB, :NB]
    w1 = w_ref[NB:, :]
    w11 = w_ref[NB:, NB:]
    r0, r1 = r_ref[0], r_ref[1]
    pan[0] = exact(r0, w00, across)
    pan[1] = exact(r0, w1[:, :NB], across) + exact(r1, w11, across)
    for k, v in ((0, exact(pan[0], w00) + exact(pan[1], w1[:, :NB])), (1, exact(pan[1], w11))):
        hi, lo = split(v)
        bhi[:, NB * k : NB * k + NB] = hi
        blo[:, NB * k : NB * k + NB] = lo

    def copy(j, i):
        return pltpu.make_async_copy(
            buf.at[j % 2, pl.ds(NB * i, NB), :], o_ref.at[i, 0, :, j, 0, :], sem.at[j % 2, i]
        )

    def body(j, carry):
        sl = pl.ds(pl.multiple_of(j * NB, NB), NB)
        hi, lo = split(t_ref[:, sl])

        @pl.when(j >= 2)
        def _():
            for i in range(row_tiles):
                copy(j - 2, i).wait()

        for i in range(row_tiles):
            rows = slice(NB * i, NB * i + NB)
            h, l = bhi[rows, :], blo[rows, :]
            buf[j % 2, rows, :] = a_ref[rows, sl] - (dot(h, hi) + (dot(h, lo) + dot(l, hi)))

        @pl.when(p <= 1)
        def _():
            buf[j % 2, :NB, :] = jnp.zeros((NB, NB), F)

        for k in range(2):

            @pl.when((j == 0) & (q == k))
            def _():
                buf[0] = pan[k]
                ri = lax.broadcasted_iota(jnp.int32, (NB, NB), 0)
                ci = lax.broadcasted_iota(jnp.int32, (NB, NB), 1)
                keep = (p > k) | ((p == k) & (ci <= ri))
                buf[0, :NB, :] = jnp.where(keep, pan[k, :NB, :], F(0))

        for i in range(row_tiles):
            copy(j, i).start()
        return carry

    lax.fori_loop(0, tiles, body, 0)
    for j in range(tiles - 2, tiles):
        for i in range(row_tiles):
            copy(j, i).wait()


def shards(kernel_tiles):
    row_tiles, _, nb, tiles, _, _ = kernel_tiles.shape
    rows, cols, lead = row_tiles * nb, tiles * nb, 2 * nb
    vmem = pl.BlockSpec(memory_space=pltpu.VMEM)
    dma = pltpu.SemaphoreType.DMA
    count = nb // 4 // 8
    a, t, r, w = pl.pallas_call(
        gather_kernel,
        out_shape=[
            jax.ShapeDtypeStruct((rows, cols), F),
            jax.ShapeDtypeStruct((lead, cols), F),
            jax.ShapeDtypeStruct((2, rows, nb), F),
            jax.ShapeDtypeStruct((lead, lead), F),
        ],
        in_specs=[pl.BlockSpec(memory_space=pltpu.HBM)],
        out_specs=[vmem] * 4,
        scratch_shapes=[
            pltpu.VMEM((lead, lead), F),
            dma((row_tiles * tiles,)),
            dma((2 * tiles + 3 + 2 * row_tiles,)),
            dma((8, 4)),
            dma((8, count)),
            dma((2,)),
            dma((2, ROW_CHUNKS)),
            dma((2,)),
            dma((1,)),
            dma((LEAD, 10)),
            dma((LEAD,)),
            dma((1,)),
            dma((1,)),
        ],
        compiler_params=pltpu.CompilerParams(
            collective_id=0, has_side_effects=True, vmem_limit_bytes=32 * 2**20
        ),
        name="gather_and_factor",
    )(kernel_tiles)
    return pl.pallas_call(
        update_kernel,
        out_shape=jax.ShapeDtypeStruct(kernel_tiles.shape, F),
        in_specs=[vmem] * 4,
        out_specs=pl.BlockSpec(memory_space=pl.ANY),
        scratch_shapes=[
            pltpu.VMEM((2, rows, nb), F),
            pltpu.VMEM((rows, lead), BF),
            pltpu.VMEM((rows, lead), BF),
            pltpu.VMEM((2, rows, nb), F),
            dma((2, row_tiles)),
        ],
        compiler_params=pltpu.CompilerParams(vmem_limit_bytes=28 * 2**20),
        name="update",
    )(a, t, r, w)


def solution(mesh):
    spec = P(None, "prow", None, None, "pcol", None)
    return jax.shard_map(shards, mesh=mesh, in_specs=(spec,), out_specs=spec, check_vma=False)
```
